128 devices in a mesh: row: 16 (over y, z), col: 8 (over x, core).
Axes of the slice: x: 4, y: 4, z: 4, core: 2. Of those that a mesh axis runs over, the one named last changes fastest.
Arguments:
- integrals: float32 [4096, 20480], P('row', 'col'), may hold values from -6 to 6
- factor: float32 [4096, 2048], P('row', 'col'), may hold values from -1 to 2, as said below
Outputs:
- coefficients: float32 [4096, 20480], P('row', 'col')
The draws below stay inside these ranges and needn't reach their ends.
Inputs may be any that keep to these rules, and one draw needn't show every extreme that they name: factor is zero above its diagonal (column index greater than row index) and between 1 and 2 on it.
All inputs are finite; a program needn't handle non-finite values.
Results may differ from the reference program's by a relative error of at most 0.0001.
Values sent between devices are 32-bit elements; how exact they have to be, the bound alone decides.
No kernel may reach another device: no remote copies, remote signals or barrier semaphores. Data moves between devices by JAX's collectives and lax.ppermute only.
A program may use at most 64 MiB of HBM per device.

```python
import jax
import jax.numpy as jnp
from jax import lax

NV = 20480
PANEL = 256
PANELS = 8
ROWS = 4096


def draw_factor(key, part):
    width_all = PANELS * PANEL
    key_noise = jax.random.fold_in(key, 17)
    key_diag = jax.random.fold_in(key, 29)
    row_ids = jnp.arange(ROWS)[:, None]
    col_ids = jnp.arange(width_all)[None, :]
    noise = jax.random.normal(key_noise, (ROWS, width_all), jnp.float32)
    same = row_ids // PANEL == col_ids // PANEL
    spread = jnp.where(same, 0.4 / PANEL ** 0.5, jnp.where(row_ids < width_all, 0.3 / width_all ** 0.5, 1.0 / width_all ** 0.5))
    diagonal = jax.random.uniform(key_diag, (ROWS, 1), jnp.float32, 1.0, 2.0)
    lower = jnp.clip(noise * spread, -0.9, 0.9)
    return jnp.where(row_ids > col_ids, lower, jnp.where(row_ids == col_ids, diagonal, 0.0)).astype(jnp.float32)


def block_scale(own_key, extent, pieces, smallest, largest):
    def one(dim, parts):
        draws = jax.random.uniform(jax.random.fold_in(jax.random.fold_in(own_key, 6), dim), (parts,), jnp.float32, smallest / len(pieces), largest / len(pieces))
        return jnp.repeat(jnp.exp(draws), extent[dim] // parts).reshape((-1,) + (1,) * (len(extent) - dim - 1))

    factor_of = one(*pieces[0])
    for cut in pieces[1:]:
        factor_of = factor_of * one(*cut)
    return factor_of


def normal_values(key, shape, scale, most, pieces=(), held_as=jnp.bfloat16):
    values = scale * jax.random.normal(key, shape, jnp.float32)
    if pieces:
        values = values * block_scale(key, shape, pieces, -0.22, 0.18)
    return jnp.clip(values, -most, most).astype(held_as)


def setup_inputs(seed: int = 0) -> dict:
    streams_of = jax.random.split(jax.random.key(seed), 3)
    integrals = normal_values(streams_of[0], (ROWS, NV), 1.0, 6.0, ((0, 16), (1, 8)), jnp.float32)
    factor = draw_factor(jax.random.fold_in(streams_of[2], 71), 0)
    return {"integrals": integrals, "factor": factor}


def reference(integrals, factor):
    work = integrals
    for panel_index in range(PANELS):
        start = panel_index * PANEL
        stop = start + PANEL
        lower_block = factor[start:stop, start:stop]
        solved = jax.scipy.linalg.solve_triangular(lower_block, work[start:stop], lower=True)
        below = work[stop:] - jnp.dot(factor[stop:, start:stop].astype(jnp.float32), solved.astype(jnp.float32), precision=lax.Precision.HIGHEST, preferred_element_type=jnp.float32)
        work = jnp.concatenate([work[:start], solved, below], axis=0)
    return work
```

```python
import jax
import jax.numpy as jnp
from jax import lax
from jax.experimental import pallas as pl
from jax.experimental.pallas import tpu as pltpu
from jax.sharding import PartitionSpec as P

F32 = jnp.float32
BF16 = jnp.bfloat16
N = 256
WIDE = 640
CHUNKS = ((0, 384), (384, 256))
TILES = {640: ((0, 256), (256, 256), (512, 128)), 384: ((0, 256), (256, 128)), 256: ((0, 256),)}


def along_y(k, sources=(0, 1, 2, 3)):
    return [(4 * y + z, 4 * ((y + k) % 4) + z) for y in sources for z in range(4)]


def along_z(k):
    return [(4 * y + z, 4 * y + (z + k) % 4) for y in range(4) for z in range(4)]


def along_x(k):
    return [(2 * x + c, 2 * ((x + k) % 4) + c) for x in range(4) for c in range(2)]


CORES = [(c, c ^ 1) for c in range(8)]


def place():
    row, col = lax.axis_index("row"), lax.axis_index("col")
    return col // 2, row // 4, row % 4, col % 2


def split(value):
    high = value.astype(BF16)
    return high, (value - high.astype(F32)).astype(BF16)


def mul(a, b):
    return lax.dot_general(a, b, (((1,), (0,)), ((), ())), preferred_element_type=F32)


def mul3(ah, al, bh, bl):
    return mul(ah, bh) + (mul(ah, bl) + mul(al, bh))


def call(kernel, outs, scratch=(), **kw):
    spec = pl.BlockSpec(memory_space=pltpu.VMEM)

    def run(*args):
        return pl.pallas_call(
            kernel,
            out_shape=outs,
            in_specs=[spec] * len(args),
            out_specs=jax.tree.map(lambda _: spec, outs),
            scratch_shapes=scratch,
            **kw,
        )(*args)

    return run


def sds(*shape, dtype=F32):
    return jax.ShapeDtypeStruct(shape, dtype)


def sort_kernel(own, y1, y2, y3, shared, rest):
    x, y, z, c = place()
    got = (own, y1, y2, y3)
    for row in range(4):
        for k in range(4):
            @pl.when(lax.rem(y - row + 4, 4) == k)
            def _():
                if row == 0:
                    @pl.when(x < 2)
                    def _():
                        shared[...] = got[k][...]
                elif row == 1:
                    rest[0:N, :] = got[k][...]

                    @pl.when(x >= 2)
                    def _():
                        shared[...] = got[k][...]
                else:
                    rest[(row - 1) * N : row * N, :] = got[k][...]


def invert_128(block):
    rows = lax.broadcasted_iota(jnp.int32, (128, 128), 0)
    cols = lax.broadcasted_iota(jnp.int32, (128, 128), 1)
    eye = rows == cols
    one = jnp.where(eye, 1.0, 0.0).astype(F32)
    scale = 1.0 / jnp.sum(jnp.where(eye, block, 0.0), axis=1, keepdims=True)
    strict = jnp.where(rows > cols, block * scale, 0.0)
    scale_row = jnp.sum(jnp.where(eye, jnp.broadcast_to(scale, (128, 128)), 0.0), axis=0, keepdims=True)
    left = [strict[8 * t : 8 * t + 8, :] for t in range(16)]
    done = [one[8 * t : 8 * t + 8, :] for t in range(16)]
    for k in range(127):
        top = k // 8
        line = jnp.broadcast_to(done[top][k % 8 : k % 8 + 1, :], (8, 128))
        for t in range(top, 16):
            done[t] = done[t] - jnp.broadcast_to(left[t][:, k : k + 1], (8, 128)) * line
    return [d * scale_row for d in done]


def invert_kernel(block, out):
    x, y, z, c = place()
    out[...] = block[...]

    @pl.when(z == 2 * lax.rem(x, 2) + c)
    def _():
        for o in (0, 128):
            for t, tile in enumerate(invert_128(block[o : o + 128, o : o + 128])):
                out[o + 8 * t : o + 8 * t + 8, o : o + 128] = tile


def copy_split(ref, at, high, low, slot, to, count):
    def step(i, _):
        o = pl.multiple_of(i * 128, 128)
        h, l = split(ref[pl.ds(at + o, 128), :])
        high[slot, pl.ds(to + o, 128), :] = h
        low[slot, pl.ds(to + o, 128), :] = l
        return 0

    lax.fori_loop(0, count // 128, step, 0)


def take_columns(pieces, first_half, at, count, high, low):
    x, y, z, c = place()
    for e in range(2):
        own, back, front, half1, half2 = pieces[5 * e : 5 * e + 5]
        middle = half1.shape[0]
        for d, ref in ((0, own), (1, back), (3, front), (2, None)):
            there = lax.rem(x - d + 4, 4)
            slot = 2 * lax.rem(there, 2) + (c if e == 0 else 1 - c)

            @pl.when((there < 2) if first_half else (there >= 2))
            def _():
                if ref is not None:
                    copy_split(ref, at, high, low, slot, 0, count)
                else:
                    n1 = min(max(middle - at, 0), count)
                    if n1:
                        copy_split(half1, at, high, low, slot, 0, n1)
                    if n1 < count:
                        copy_split(half2, at + n1 - middle, high, low, slot, n1, count - n1)


def take_rows(pieces, panels):
    x, y, z, c = place()
    own, back, front, half1, half2 = pieces
    panels[z] = own[...]
    panels[lax.rem(z + 3, 4)] = back[...]
    panels[lax.rem(z + 1, 4)] = front[...]
    two = lax.rem(z + 2, 4)
    panels[two, 0:128, :] = half1[...]
    panels[two, 128:256, :] = half2[...]


def solve_quarter(high, low, panels, xh, xl, first, own, wide):
    x, y, z, c = place()

    def block(i, j, r, q, rows=128, cols=128):
        at = pl.multiple_of(lax.rem(z - i + 4, 4) * N + r, 128)
        return high[j, pl.ds(at, rows), q : q + cols], low[j, pl.ds(at, rows), q : q + cols]

    for i in range(4):
        for o, n in TILES[wide]:
            lanes = slice(o, o + n)
            value = panels[i, :, lanes]
            for j in range(i):
                bh, bl = block(i, j, 0, 0, N, N)
                to = (first + j) * N
                value = value - mul3(bh, bl, xh[to : to + N, lanes], xl[to : to + N, lanes])
            top, bottom = value[:128], value[128:]
            top = mul3(*block(i, i, 0, 0), *split(top))
            th, tl = split(top)
            bottom = bottom - mul3(*block(i, i, 128, 0), th, tl)
            bottom = mul3(*block(i, i, 128, 128), *split(bottom))
            bh, bl = split(bottom)
            to = (first + i) * N
            xh[to : to + 128, lanes] = th
            xl[to : to + 128, lanes] = tl
            xh[to + 128 : to + N, lanes] = bh
            xl[to + 128 : to + N, lanes] = bl

            @pl.when(z == i)
            def _():
                own[0:128, lanes] = top
                own[128:256, lanes] = bottom


def first_kernel(*refs):
    tri, rest, sides, second = refs[0:10], refs[10:20], refs[20:25], refs[25]
    xh, xl, own, work = refs[26:30]
    high, low, dh, dl, panels = refs[30:]
    take_columns(tri, True, 0, 1024, high, low)
    take_columns(rest, True, 0, N, dh, dl)
    take_rows(sides, panels)
    solve_quarter(high, low, panels, xh, xl, 0, own, WIDE)
    for o, n in TILES[WIDE]:
        lanes = slice(o, o + n)
        value = second[:, lanes]
        for j in range(4):
            value = value - mul3(dh[j], dl[j], xh[j * N : j * N + N, lanes], xl[j * N : j * N + N, lanes])
        work[:, lanes] = value


def partial_kernel(*refs):
    rest, (xh, xl), out, high, low = refs[0:10], refs[10:12], refs[12], refs[13], refs[14]
    take_columns(rest, True, N, 2 * N, high, low)
    for o, n in TILES[WIDE]:
        lanes = slice(o, o + n)
        value = None
        for j in range(4):
            part = mul3(high[j], low[j], xh[j * N : j * N + N, lanes], xl[j * N : j * N + N, lanes])
            value = part if value is None else value + part
        out[:, lanes] = value


def second_kernel(start, wide):
    def kernel(*refs):
        tri, rest, sides, (own_first, part) = refs[0:10], refs[10:20], refs[20:25], refs[25:27]
        outs = refs[27:31]
        high, low, lh, ll, panels, xh, xl, own = refs[31:]
        x, y, z, c = place()
        take_columns(tri, False, 0, 1024, high, low)
        take_columns(rest, False, N, 2 * N, lh, ll)
        take_rows(sides, panels)
        solve_quarter(high, low, panels, xh, xl, 0, own, wide)

        def give(row, lanes, value):
            for k in range(4):
                @pl.when(lax.rem(row - y + 4, 4) == k)
                def _():
                    outs[k][:, lanes] = value

        whole = slice(0, wide)
        give(0, whole, own_first[:, start : start + wide])
        give(1, whole, own[...])
        for o, n in TILES[wide]:
            lanes = slice(o, o + n)
            for row in range(2):
                value = part[row * N : row * N + N, start + o : start + o + n]
                for j in range(4):
                    value = value + mul3(
                        lh[j, row * N : row * N + N],
                        ll[j, row * N : row * N + N],
                        xh[j * N : j * N + N, lanes],
                        xl[j * N : j * N + N, lanes],
                    )
                give(2 + row, lanes, value)

    return kernel


def last_kernel(*refs):
    mine, got, out = refs[0], refs[1:-1], refs[-1]
    x, y, z, c = place()
    for q, (start, wide) in enumerate(CHUNKS):
        for chunk in range(4):
            lanes = slice(chunk * WIDE + start, chunk * WIDE + start + wide)
            for k in range(4):
                @pl.when(lax.rem(y - chunk + 4, 4) == k)
                def _():
                    @pl.when(y < 2)
                    def _():
                        out[:, lanes] = got[4 * q + k][...]

                    @pl.when(y >= 2)
                    def _():
                        out[:, lanes] = mine[:, lanes] - got[4 * q + k][...]


def gather_ring(value, axis, shift):
    half = value.shape[0] // 2
    back = lax.ppermute(value, axis, shift(1))
    front = lax.ppermute(value, axis, shift(3))
    half1 = lax.ppermute(back[:half], axis, shift(1))
    half2 = lax.ppermute(front[half:], axis, shift(3))
    return [value, back, front, half1, half2]


def both_cores(pieces):
    return pieces + [lax.ppermute(p, "col", CORES) for p in pieces]


def shards(integrals, factor):
    x, y, z, c = place()
    got = [lax.ppermute(factor, "row", along_y(k)) for k in (1, 2, 3)]
    chunk = lambda q: integrals[:, q * WIDE : (q + 1) * WIDE]
    from0 = [lax.ppermute(chunk(k), "row", along_y(k, (0,))) for k in (1, 2, 3)]
    from1 = [lax.ppermute(chunk((k + 1) % 4), "row", along_y(k, (1,))) for k in (1, 2, 3)]
    shared, rest = call(sort_kernel, (sds(N, N), sds(3 * N, N)))(factor, *got)
    rest = both_cores(gather_ring(rest, "col", along_x))
    shared = call(invert_kernel, sds(N, N))(shared)
    tri = jnp.concatenate([shared] + [lax.ppermute(shared, "row", along_z(k)) for k in (1, 2, 3)], axis=0)
    tri = both_cores(gather_ring(tri, "col", along_x))
    side1 = jnp.where(y == 0, chunk(0), from0[0] + from0[1] + from0[2])
    side2 = jnp.where(y == 1, chunk(1), from1[0] + from1[1] + from1[2])
    sides = gather_ring(side1, "row", along_z)
    quarter = [pltpu.VMEM((4, 4 * N, N), BF16)] * 2
    xh, xl, own, work = call(
        first_kernel,
        (sds(4 * N, WIDE, dtype=BF16), sds(4 * N, WIDE, dtype=BF16), sds(N, WIDE), sds(N, WIDE)),
        quarter + [pltpu.VMEM((4, N, N), BF16)] * 2 + [pltpu.VMEM((4, N, WIDE), F32)],
    )(*tri, *rest, *sides, side2)
    works = [gather_ring(work[:, o : o + n], "row", along_z) for o, n in CHUNKS]
    part = call(partial_kernel, sds(2 * N, WIDE), [pltpu.VMEM((4, 2 * N, N), BF16)] * 2)(*rest, xh, xl)
    back = []
    for (o, n), sides in zip(CHUNKS, works):
        outs = call(
            second_kernel(o, n),
            (sds(N, n),) * 4,
            quarter
            + [pltpu.VMEM((4, 2 * N, N), BF16)] * 2
            + [pltpu.VMEM((4, N, n), F32)]
            + [pltpu.VMEM((4 * N, n), BF16)] * 2
            + [pltpu.VMEM((N, n), F32)],
        )(*tri, *rest, *sides, own, part)
        back += [outs[0]] + [lax.ppermute(outs[k], "row", along_y(k)) for k in (1, 2, 3)]
    return call(last_kernel, sds(*integrals.shape))(integrals, *back)


def solution(mesh):
    placed = (P("row", "col"), P("row", "col"))
    return jax.shard_map(
        shards, mesh=mesh, in_specs=placed, out_specs=P("row", "col"), check_vma=False
    )
```

```python
import jax
import jax.numpy as jnp
from jax import lax
from jax.experimental import pallas as pl
from jax.experimental.pallas import tpu as pltpu
from jax.sharding import PartitionSpec as P


F32 = jnp.float32
BF16 = jnp.bfloat16
N = 256
WIDE = 640
ANYWHERE = pltpu.HBM
CHUNKS = ((0, 256), (256, 384))
TILES = {640: ((0, 256), (256, 256), (512, 128)), 384: ((0, 256), (256, 128)), 256: ((0, 256),)}


def along_y(k, sources=(0, 1, 2, 3)):
    return [(4 * y + z, 4 * ((y + k) % 4) + z) for y in sources for z in range(4)]


def along_z(k):
    return [(4 * y + z, 4 * y + (z + k) % 4) for y in range(4) for z in range(4)]


def along_x(k):
    return [(2 * x + c, 2 * ((x + k) % 4) + c) for x in range(4) for c in range(2)]


CORES = [(c, c ^ 1) for c in range(8)]


def place():
    row, col = lax.axis_index("row"), lax.axis_index("col")
    return col // 2, row // 4, row % 4, col % 2


def split(value):
    high = value.astype(BF16)
    return high, (value - high.astype(F32)).astype(BF16)


def mul(a, b):
    return lax.dot_general(a, b, (((1,), (0,)), ((), ())), preferred_element_type=F32)


def mul3(ah, al, bh, bl):
    return mul(ah, bh) + (mul(ah, bl) + mul(al, bh))


def call(kernel, outs, scratch=(), space=pltpu.VMEM, **kw):
    spec = pl.BlockSpec(memory_space=pltpu.VMEM)

    def run(*args):
        return pl.pallas_call(
            kernel,
            out_shape=outs,
            in_specs=[pl.BlockSpec(memory_space=space)] * len(args),
            out_specs=jax.tree.map(lambda _: spec, outs),
            scratch_shapes=scratch,
            **kw,
        )(*args)

    return run


class Copies:
    def __init__(self, sems):
        self.sems, self.used, self.by_key = sems, 0, {}

    def start(self, key, source, target, when=None):
        copy = pltpu.make_async_copy(source, target, self.sems.at[self.used])
        self.used += 1
        self.by_key.setdefault(key, []).append((copy, when))
        if when is None:
            copy.start()
        else:
            pl.when(when)(copy.start)

    def wait(self, key):
        for copy, when in self.by_key.pop(key):
            if when is None:
                copy.wait()
            else:
                pl.when(when)(copy.wait)


def sds(*shape, dtype=F32):
    return jax.ShapeDtypeStruct(shape, dtype)


def sort_kernel(own, y1, y2, y3, shared, rest):
    x, y, _, _ = place()
    got = (own, y1, y2, y3)
    for row in range(4):
        for k in range(4):
            @pl.when(lax.rem(y - row + 4, 4) == k)
            def _():
                if row:
                    rest[(row - 1) * N : row * N, :] = got[k][...]
                if row < 2:
                    @pl.when((x < 2) if row == 0 else (x >= 2))
                    def _():
                        shared[...] = got[k][...]


def invert_kernel(block, out, strict):
    x, _, z, c = place()
    out[...] = block[...]

    @pl.when(z == 2 * lax.rem(x, 2) + c)
    def _():
        rows = lax.broadcasted_iota(jnp.int32, (128, 128), 0)
        cols = lax.broadcasted_iota(jnp.int32, (128, 128), 1)
        eye = rows == cols
        one = jnp.where(eye, 1.0, 0.0).astype(F32)
        scale_row, done = [], []
        for b in range(2):
            value = block[128 * b : 128 * b + 128, 128 * b : 128 * b + 128]
            scale = 1.0 / jnp.sum(jnp.where(eye, value, 0.0), axis=1, keepdims=True)
            strict[b] = jnp.where(rows > cols, value * scale, 0.0)
            scale_row.append(jnp.sum(jnp.where(eye, jnp.broadcast_to(scale, (128, 128)), 0.0), axis=0, keepdims=True))
            done.append([one[8 * t : 8 * t + 8, :] for t in range(16)])
        for k in range(127):
            first = (k + 1) // 8
            for b in range(2):
                line = jnp.broadcast_to(done[b][k // 8][k % 8 : k % 8 + 1, :], (8, 128))
                for t in range(first, 16):
                    left = strict[b, 8 * t : 8 * t + 8, :]
                    done[b][t] = done[b][t] - jnp.broadcast_to(left[:, k : k + 1], (8, 128)) * line
        for b in range(2):
            for t in range(16):
                at = 128 * b + 8 * t
                out[at : at + 8, 128 * b : 128 * b + 128] = done[b][t] * scale_row[b]


def stack_kernel(own, z1, z2, z3, a, b):
    a[0:256, :] = own[...]
    a[256:512, :] = z1[...]
    b[0:256, :] = z2[...]
    b[256:512, :] = z3[...]


def fetch_columns(copies, key, pieces, first_half, at, count, target):
    x, _, _, c = place()
    for e in range(2):
        own, back, front, half_a, half_b = pieces[5 * e : 5 * e + 5]
        for d, ref in ((0, own), (1, back), (3, front), (2, None)):
            there = lax.rem(x - d + 4, 4)
            slot = 2 * lax.rem(there, 2) + (c if e == 0 else 1 - c)
            when = (there < 2) if first_half else (there >= 2)
            if ref is not None:
                copies.start(key, ref.at[at : at + count], target.at[slot], when)
                continue
            middle = half_a.shape[0]
            n1 = min(max(middle - at, 0), count)
            if n1:
                copies.start(key, half_a.at[at : at + n1], target.at[slot, 0:n1], when)
            if n1 < count:
                o = at + n1 - middle
                copies.start(key, half_b.at[o : o + count - n1], target.at[slot, n1:count], when)


def fetch_sides(copies, key, sides, panels):
    _, _, z, _ = place()
    for k, ref in enumerate(sides):
        copies.start(key, ref, panels.at[lax.rem(z - k + 4, 4)])


def split_kernel(*refs):
    count = len(refs) // 3
    for k in range(count):
        def step(i, _):
            rows = pl.ds(pl.multiple_of(i * 128, 128), 128)
            refs[count + 2 * k][rows, :], refs[count + 2 * k + 1][rows, :] = split(refs[k][rows, :])
            return 0

        lax.fori_loop(0, refs[k].shape[0] // 128, step, 0)


def fetch_quarter(copies, key, early, late, first_half, high, low):
    x, _, _, c = place()
    for e in range(2):
        for q, d in enumerate((0, 1, 3, 2)):
            if d == 2 and late is None:
                continue
            there = lax.rem(x - d + 4, 4)
            slot = 2 * lax.rem(there, 2) + (c if e == 0 else 1 - c)
            when = (there < 2) if first_half else (there >= 2)
            pieces = late[4 * e :] if d == 2 else early[12 * e + 4 * q :]
            for h in range(2):
                for ref, target in zip(pieces[2 * h : 2 * h + 2], (high, low)):
                    copies.start(key, ref, target.at[slot, 512 * h : 512 * h + 512], when)


def split_rows(raw, high, low, first=0):
    for j in range(4):
        lanes = slice((first + j) * N, (first + j + 1) * N)

        def step(i, _):
            rows = pl.ds(pl.multiple_of(i * 128, 128), 128)
            high[rows, lanes], low[rows, lanes] = split(raw[j, rows, :])
            return 0

        lax.fori_loop(0, raw.shape[1] // 128, step, 0)


def prepare_rows_kernel(*refs):
    dh, dl, lh, ll, raw_d, raw1, raw2, sems = refs[10:]
    copies = Copies(sems)
    fetch_columns(copies, 0, refs[:10], True, 0, N, raw_d)
    fetch_columns(copies, 1, refs[:10], True, N, 2 * N, raw1)
    fetch_columns(copies, 2, refs[:10], False, N, 2 * N, raw2)
    copies.wait(0)
    split_rows(raw_d, dh, dl)
    copies.wait(1)
    split_rows(raw1, lh, ll)
    copies.wait(2)
    split_rows(raw2, lh, ll, 4)


def solve_quarter(high, low, panels, xh, xl, wide, extra):
    _, _, z, _ = place()

    def block(i, j, r=0, q=0, rows=N, cols=N):
        at = pl.multiple_of(lax.rem(z - i + 4, 4) * N + r, 128)
        return high[j, pl.ds(at, rows), q : q + cols], low[j, pl.ds(at, rows), q : q + cols]

    def update(i, j, lanes):
        d = slice(j * N, j * N + N)
        panels[i, :, lanes] -= mul3(*block(i, j), xh[d, lanes], xl[d, lanes])

    def top(i, lanes):
        d = i * N
        value = mul3(*block(i, i, 0, 0, 128, 128), *split(panels[i, 0:128, lanes]))
        panels[i, 0:128, lanes] = value
        xh[d : d + 128, lanes], xl[d : d + 128, lanes] = split(value)

    def middle(i, lanes):
        d = slice(i * N, i * N + 128)
        panels[i, 128:256, lanes] -= mul3(*block(i, i, 128, 0, 128, 128), xh[d, lanes], xl[d, lanes])

    def bottom(i, lanes):
        d = i * N + 128
        value = mul3(*block(i, i, 128, 128, 128, 128), *split(panels[i, 128:256, lanes]))
        panels[i, 128:256, lanes] = value
        xh[d : d + 128, lanes], xl[d : d + 128, lanes] = split(value)

    tiles = [slice(o, o + n) for o, n in TILES[wide]]
    for i in range(4):
        spare = [lambda t, k=k: update(k, i - 1, t) for k in range(i + 1, 4) if i]
        if i:
            spare.append(lambda t: extra(i - 1, t))
        for k, step in enumerate((top, middle, bottom)):
            for lanes in tiles:
                if k == 0 and i:
                    update(i, i - 1, lanes)
                step(i, lanes)
            for work in spare[k : None if k == 2 else k + 1]:
                for lanes in tiles:
                    work(lanes)
    for lanes in tiles:
        extra(3, lanes)


def first_kernel(*refs):
    early, late, (dh, dl), sides, second = refs[:24], refs[24:28], refs[28:30], refs[30:34], refs[34:38]
    (xh, xl, own), works = refs[38:41], refs[41 : 41 + len(CHUNKS)]
    high, low, dhv, dlv, panels, mine, raw, sems = refs[41 + len(CHUNKS) :]
    x, y, z, c = place()
    far = x >= 2
    copies = Copies(sems)
    for e in range(2):
        for h in range(2):
            copies.start(1, late[2 * e + h], raw.at[e, 512 * h : 512 * h + 512], far)
    fetch_sides(copies, 0, sides, panels)
    fetch_quarter(copies, 0, early, None, True, high, low)
    copies.start(0, dh, dhv)
    copies.start(0, dl, dlv)
    for k, ref in enumerate(second):
        copies.start(0, ref, mine, y == k)
    copies.wait(1)

    @pl.when(far)
    def _():
        for e in range(2):
            slot = 2 * lax.rem(x, 2) + (c if e == 0 else 1 - c)

            def step(i, _):
                rows = pl.ds(pl.multiple_of(i * 128, 128), 128)
                high[slot, rows, :], low[slot, rows, :] = split(raw[e, rows, :])
                return 0

            lax.fori_loop(0, 8, step, 0)

    copies.wait(0)

    def extra(j, lanes):
        d = slice(j * N, j * N + N)
        mine[:, lanes] -= mul3(dhv[:, d], dlv[:, d], xh[d, lanes], xl[d, lanes])

    solve_quarter(high, low, panels, xh, xl, WIDE, extra)
    own[...] = panels[z]
    for (o, n), work in zip(CHUNKS, works):
        work[...] = mine[:, o : o + n]


def partial_kernel(lh, ll, xh, xl, out, lhv, llv, xhv, xlv, sems):
    copies = Copies(sems)
    copies.start(0, xh, xhv)
    copies.start(0, xl, xlv)
    copies.start(0, lh.at[:, 0 : 4 * N], lhv)
    copies.start(0, ll.at[:, 0 : 4 * N], llv)
    copies.wait(0)

    def step(i, _):
        rows = pl.ds(pl.multiple_of(i * N, N), N)
        for o, n in TILES[WIDE]:
            lanes = slice(o, o + n)
            out[rows, lanes] = mul3(lhv[rows, :], llv[rows, :], xhv[:, lanes], xlv[:, lanes])
        return 0

    lax.fori_loop(0, 2, step, 0)


def second_kernel(start, wide):
    def kernel(*refs):
        early, late, (lh, ll), sides = refs[:24], refs[24:32], refs[32:34], refs[34:38]
        own_first, part = refs[38:40]
        outs = refs[40:44]
        high, low, lhv, llv, panels, result, xh, xl, sems = refs[44:]
        _, y, z, _ = place()
        copies = Copies(sems)
        fetch_sides(copies, 0, sides, panels)
        fetch_quarter(copies, 0, early, late, False, high, low)
        copies.start(0, own_first.at[:, start : start + wide], result.at[0])
        copies.start(0, lh.at[:, 4 * N : 8 * N], lhv)
        copies.start(0, ll.at[:, 4 * N : 8 * N], llv)
        for r in range(2):
            copies.start(0, part.at[r * N : r * N + N, start : start + wide], result.at[2 + r])
        copies.wait(0)

        def extra(j, lanes):
            d = slice(j * N, j * N + N)
            for r in range(2):
                rows = slice(r * N, r * N + N)
                result[2 + r, :, lanes] += mul3(lhv[rows, d], llv[rows, d], xh[d, lanes], xl[d, lanes])

        solve_quarter(high, low, panels, xh, xl, wide, extra)
        result[1] = panels[z]
        for k in range(4):
            outs[k][...] = result[lax.rem(y + k, 4)]

    return kernel


def last_kernel(start, wide):
    def kernel(mine, got0, got1, got2, got3, *refs):
        out, kept, sems = refs[-3:]
        _, y, _, _ = place()
        copies = Copies(sems)
        for chunk in range(4):
            lanes = slice(chunk * WIDE + start, chunk * WIDE + start + wide)
            copies.start(0, mine.at[:, lanes], kept.at[chunk], y >= 2)
        copies.wait(0)
        for k, got in enumerate((got0, got1, got2, got3)):
            chunk = lax.rem(y - k + 4, 4)

            @pl.when(y < 2)
            def _():
                kept[chunk] = got[...]

            @pl.when(y >= 2)
            def _():
                kept[chunk] = kept[chunk] - got[...]

        for chunk in range(4):
            lanes = slice(chunk * WIDE + start, chunk * WIDE + start + wide)
            copies.start(1, kept.at[chunk], out.at[:, lanes])
        copies.wait(1)

    return kernel


def send(value, axis, pairs):
    return lax.ppermute(value, axis, pairs)


def gather_x(a, b):
    back = [send(v, "col", along_x(1)) for v in (a, b)]
    front = [send(v, "col", along_x(3)) for v in (a, b)]
    far = [send(back[0], "col", along_x(1)), send(front[1], "col", along_x(3))]
    pieces = [a, b, *back, *front, *far]
    return pieces + [send(p, "col", CORES) for p in pieces]


def gather_x_whole(value):
    half = value.shape[0] // 2
    back = send(value, "col", along_x(1))
    front = send(value, "col", along_x(3))
    far = [send(back[:half], "col", along_x(1)), send(front[half:], "col", along_x(3))]
    pieces = [value, back, front, *far]
    return pieces + [send(p, "col", CORES) for p in pieces]


def gather_z(value):
    return [value] + [send(value, "row", along_z(k)) for k in (1, 2, 3)]


def work_on(integrals, factor):
    _, y, _, _ = place()
    bf = lambda *shape: sds(*shape, dtype=BF16)
    vf = lambda *shape: pltpu.VMEM(shape, F32)
    vb = lambda *shape: pltpu.VMEM(shape, BF16)
    sems = pltpu.SemaphoreType.DMA((64,))
    got = [send(factor, "row", along_y(k)) for k in (1, 2, 3)]
    chunks = [integrals[:, q * WIDE : (q + 1) * WIDE] for q in range(4)]
    mine = (chunks[0], chunks[1], *(jnp.where(y == 0, chunks[k], chunks[(k + 1) % 4]) for k in (1, 2, 3)))
    mine = lax.optimization_barrier(mine)
    came = [send(mine[k + 1], "row", along_y(k, (0, 1))) for k in (1, 2, 3)]
    shared, rest = call(sort_kernel, (sds(N, N), sds(3 * N, N)))(factor, *got)
    rest = gather_x_whole(rest)
    shared = call(invert_kernel, sds(N, N), [vf(2, 128, 128)])(shared)
    tri = gather_x(*call(stack_kernel, (sds(2 * N, N), sds(2 * N, N)))(*gather_z(shared)))
    side1 = jnp.where(y == 0, mine[0], jnp.where(y == 1, came[0], jnp.where(y == 2, came[1], came[2])))
    sides = gather_z(side1)
    side2 = (came[2], mine[1], came[0], came[1])
    dh, dl, lh, ll = call(
        prepare_rows_kernel,
        (bf(N, 4 * N), bf(N, 4 * N), bf(2 * N, 8 * N), bf(2 * N, 8 * N)),
        [vf(4, N, N), vf(4, 2 * N, N), vf(4, 2 * N, N), sems],
        ANYWHERE,
    )(*rest)
    early = call(split_kernel, (bf(2 * N, N),) * 24)(*tri[0:6], *tri[8:14])
    quarter = [vb(4, 4 * N, N), vb(4, 4 * N, N)]
    xh, xl, own, *works = call(
        first_kernel,
        (bf(4 * N, WIDE), bf(4 * N, WIDE), sds(N, WIDE)) + tuple(sds(N, n) for _, n in CHUNKS),
        quarter + [vb(N, 4 * N), vb(N, 4 * N), vf(4, N, WIDE), vf(N, WIDE), vf(2, 4 * N, N), sems],
        ANYWHERE,
    )(*early, *tri[6:8], *tri[14:16], dh, dl, *sides, *side2)
    late = call(split_kernel, (bf(2 * N, N),) * 8)(*tri[6:8], *tri[14:16])
    works = [gather_z(work) for work in works]
    part = call(
        partial_kernel,
        sds(2 * N, WIDE),
        [vb(2 * N, 4 * N), vb(2 * N, 4 * N), vb(4 * N, WIDE), vb(4 * N, WIDE), sems],
        ANYWHERE,
    )(lh, ll, xh, xl)
    out = ()
    for q, (o, n) in enumerate(CHUNKS):
        outs = call(
            second_kernel(o, n),
            (sds(N, n),) * 4,
            quarter
            + [vb(2 * N, 4 * N), vb(2 * N, 4 * N), vf(4, N, n), vf(4, N, n), vb(4 * N, n), vb(4 * N, n), sems],
            ANYWHERE,
        )(*early, *late, lh, ll, *works[q], own, part)
        got = [outs[0]] + [send(outs[k], "row", along_y(k)) for k in (1, 2, 3)]
        out = (finish(o, n, integrals, got, out),)
    return out[0]


def finish(start, wide, integrals, got, out):
    anywhere, inside = pl.BlockSpec(memory_space=ANYWHERE), pl.BlockSpec(memory_space=pltpu.VMEM)
    return pl.pallas_call(
        last_kernel(start, wide),
        out_shape=sds(*integrals.shape),
        in_specs=[anywhere] + [inside] * 4 + [anywhere] * len(out),
        out_specs=anywhere,
        scratch_shapes=[pltpu.VMEM((4, N, wide), F32), pltpu.SemaphoreType.DMA((8,))],
        input_output_aliases={5: 0} if out else {},
    )(integrals, *got, *out)


def solution(mesh):
    placed = (P("row", "col"), P("row", "col"))
    return jax.shard_map(work_on, mesh=mesh, in_specs=placed, out_specs=P("row", "col"), check_vma=False)
```

```python
import jax
import jax.numpy as jnp
from jax import lax
from jax.experimental import pallas as pl
from jax.experimental.pallas import tpu as pltpu
from jax.sharding import PartitionSpec as P


F32 = jnp.float32
BF16 = jnp.bfloat16
N = 256
WIDE = 640
ANYWHERE = pltpu.HBM
CHUNKS = ((0, 256), (256, 384))
TILES = {640: ((0, 256), (256, 256), (512, 128)), 384: ((0, 256), (256, 128)), 256: ((0, 256),)}


def along_y(k, sources=(0, 1, 2, 3)):
    return [(4 * y + z, 4 * ((y + k) % 4) + z) for y in sources for z in range(4)]


def along_z(k):
    return [(4 * y + z, 4 * y + (z + k) % 4) for y in range(4) for z in range(4)]


def along_x(k):
    return [(2 * x + c, 2 * ((x + k) % 4) + c) for x in range(4) for c in range(2)]


CORES = [(c, c ^ 1) for c in range(8)]


def place():
    row, col = lax.axis_index("row"), lax.axis_index("col")
    return col // 2, row // 4, row % 4, col % 2


def split(value):
    high = value.astype(BF16)
    return high, (value - high.astype(F32)).astype(BF16)


def mul(a, b):
    return lax.dot_general(a, b, (((1,), (0,)), ((), ())), preferred_element_type=F32)


def mul3(ah, al, bh, bl):
    both = mul(jnp.concatenate([ah, al], axis=0), bh)
    return both[: ah.shape[0]] + (mul(ah, bl) + both[ah.shape[0] :])


def call(kernel, outs, scratch=(), space=pltpu.VMEM, **kw):
    spec = pl.BlockSpec(memory_space=pltpu.VMEM)

    def run(*args):
        return pl.pallas_call(
            kernel,
            out_shape=outs,
            in_specs=[pl.BlockSpec(memory_space=space)] * len(args),
            out_specs=jax.tree.map(lambda _: spec, outs),
            scratch_shapes=scratch,
            **kw,
        )(*args)

    return run


class Copies:
    def __init__(self, sems):
        self.sems, self.used, self.by_key = sems, 0, {}

    def start(self, key, source, target, when=None):
        copy = pltpu.make_async_copy(source, target, self.sems.at[self.used])
        self.used += 1
        self.by_key.setdefault(key, []).append((copy, when))
        if when is None:
            copy.start()
        else:
            pl.when(when)(copy.start)

    def wait(self, key):
        for copy, when in self.by_key.pop(key, ()):
            if when is None:
                copy.wait()
            else:
                pl.when(when)(copy.wait)


def sds(*shape, dtype=F32):
    return jax.ShapeDtypeStruct(shape, dtype)


def sort_kernel(own, y1, y2, y3, shared, rest):
    x, y, _, _ = place()
    got = (own, y1, y2, y3)
    for row in range(4):
        for k in range(4):
            @pl.when(lax.rem(y - row + 4, 4) == k)
            def _():
                if row:
                    rest[(row - 1) * N : row * N, :] = got[k][...]
                if row < 2:
                    @pl.when((x < 2) if row == 0 else (x >= 2))
                    def _():
                        shared[...] = got[k][...]


def invert_kernel(block, out, strict):
    x, _, z, c = place()
    out[...] = block[...]

    @pl.when(z == 2 * lax.rem(x, 2) + c)
    def _():
        rows = lax.broadcasted_iota(jnp.int32, (128, 128), 0)
        cols = lax.broadcasted_iota(jnp.int32, (128, 128), 1)
        eye = rows == cols
        one = jnp.where(eye, 1.0, 0.0).astype(F32)
        scale_row, done = [], []
        for b in range(2):
            value = block[128 * b : 128 * b + 128, 128 * b : 128 * b + 128]
            scale = 1.0 / jnp.sum(jnp.where(eye, value, 0.0), axis=1, keepdims=True)
            strict[b] = jnp.where(rows > cols, value * scale, 0.0)
            scale_row.append(jnp.sum(jnp.where(eye, jnp.broadcast_to(scale, (128, 128)), 0.0), axis=0, keepdims=True))
            done.append([one[8 * t : 8 * t + 8, :] for t in range(16)])
        for k in range(127):
            first = (k + 1) // 8
            for b in range(2):
                line = jnp.broadcast_to(done[b][k // 8][k % 8 : k % 8 + 1, :], (8, 128))
                for t in range(first, 16):
                    left = strict[b, 8 * t : 8 * t + 8, :]
                    done[b][t] = done[b][t] - jnp.broadcast_to(left[:, k : k + 1], (8, 128)) * line
        for b in range(2):
            for t in range(16):
                at = 128 * b + 8 * t
                out[at : at + 8, 128 * b : 128 * b + 128] = done[b][t] * scale_row[b]


def stack_kernel(own, z1, z2, z3, a, b):
    a[0:256, :] = own[...]
    a[256:512, :] = z1[...]
    b[0:256, :] = z2[...]
    b[256:512, :] = z3[...]


def fetch_columns(copies, key, pieces, first_half, at, count, target):
    x, _, _, c = place()
    for e in range(2):
        own, back, front, half_a, half_b = pieces[5 * e : 5 * e + 5]
        for d, ref in ((0, own), (1, back), (3, front), (2, None)):
            there = lax.rem(x - d + 4, 4)
            slot = 2 * lax.rem(there, 2) + (c if e == 0 else 1 - c)
            when = (there < 2) if first_half else (there >= 2)
            if ref is not None:
                copies.start(key, ref.at[at : at + count], target.at[slot], when)
                continue
            middle = half_a.shape[0]
            n1 = min(max(middle - at, 0), count)
            if n1:
                copies.start(key, half_a.at[at : at + n1], target.at[slot, 0:n1], when)
            if n1 < count:
                o = at + n1 - middle
                copies.start(key, half_b.at[o : o + count - n1], target.at[slot, n1:count], when)


def fetch_sides(copies, key, sides, panels):
    _, _, z, _ = place()
    for k, ref in enumerate(sides):
        copies.start(key, ref, panels.at[lax.rem(z - k + 4, 4)])


def split_kernel(*refs):
    count = len(refs) // 3
    for k in range(count):
        def step(i, _):
            rows = pl.ds(pl.multiple_of(i * 128, 128), 128)
            refs[count + 2 * k][rows, :], refs[count + 2 * k + 1][rows, :] = split(refs[k][rows, :])
            return 0

        lax.fori_loop(0, refs[k].shape[0] // 128, step, 0)


def fetch_quarter(copies, key, early, late, first_half, high, low):
    x, _, _, c = place()
    for e in range(2):
        for q, d in enumerate((0, 1, 3, 2)):
            if d == 2 and late is None:
                continue
            there = lax.rem(x - d + 4, 4)
            slot = 2 * lax.rem(there, 2) + (c if e == 0 else 1 - c)
            when = (there < 2) if first_half else (there >= 2)
            pieces = late[4 * e :] if d == 2 else early[12 * e + 4 * q :]
            for h in range(2):
                for ref, target in zip(pieces[2 * h : 2 * h + 2], (high, low)):
                    copies.start(key, ref, target.at[slot, 512 * h : 512 * h + 512], when)


def split_rows(raw, high, low, first=0):
    for j in range(4):
        lanes = slice((first + j) * N, (first + j + 1) * N)

        def step(i, _):
            rows = pl.ds(pl.multiple_of(i * 128, 128), 128)
            high[rows, lanes], low[rows, lanes] = split(raw[j, rows, :])
            return 0

        lax.fori_loop(0, raw.shape[1] // 128, step, 0)


def prepare_rows_kernel(*refs):
    dh, dl, lh, ll, raw_d, raw1, raw2, sems = refs[10:]
    copies = Copies(sems)
    fetch_columns(copies, 0, refs[:10], True, 0, N, raw_d)
    fetch_columns(copies, 1, refs[:10], True, N, 2 * N, raw1)
    fetch_columns(copies, 2, refs[:10], False, N, 2 * N, raw2)
    copies.wait(0)
    split_rows(raw_d, dh, dl)
    copies.wait(1)
    split_rows(raw1, lh, ll)
    copies.wait(2)
    split_rows(raw2, lh, ll, 4)


def solve_quarter(high, low, panels, xh, xl, wide, extra):
    _, _, z, _ = place()

    def block(i, j, r=0, q=0, rows=N, cols=N):
        at = pl.multiple_of(lax.rem(z - i + 4, 4) * N + r, 128)
        return high[j, pl.ds(at, rows), q : q + cols], low[j, pl.ds(at, rows), q : q + cols]

    def update(i, j, lanes):
        d = slice(j * N, j * N + N)
        panels[i, :, lanes] -= mul3(*block(i, j), xh[d, lanes], xl[d, lanes])

    def top(i, lanes):
        d = i * N
        value = mul3(*block(i, i, 0, 0, 128, 128), *split(panels[i, 0:128, lanes]))
        panels[i, 0:128, lanes] = value
        xh[d : d + 128, lanes], xl[d : d + 128, lanes] = split(value)

    def middle(i, lanes):
        d = slice(i * N, i * N + 128)
        panels[i, 128:256, lanes] -= mul3(*block(i, i, 128, 0, 128, 128), xh[d, lanes], xl[d, lanes])

    def bottom(i, lanes):
        d = i * N + 128
        value = mul3(*block(i, i, 128, 128, 128, 128), *split(panels[i, 128:256, lanes]))
        panels[i, 128:256, lanes] = value
        xh[d : d + 128, lanes], xl[d : d + 128, lanes] = split(value)

    tiles = [slice(o, o + n) for o, n in TILES[wide]]
    for i in range(4):
        spare = [lambda t, k=k: update(k, i - 1, t) for k in range(i + 1, 4) if i]
        if i:
            spare.append(lambda t: extra(i - 1, t))
        for k, step in enumerate((top, middle, bottom)):
            for lanes in tiles:
                if k == 0 and i:
                    update(i, i - 1, lanes)
                step(i, lanes)
            for work in spare[k : None if k == 2 else k + 1]:
                for lanes in tiles:
                    work(lanes)
    for lanes in tiles:
        extra(3, lanes)


def first_kernel(*refs):
    early, late, (dh, dl), sides, second = refs[:24], refs[24:28], refs[28:30], refs[30:34], refs[34:38]
    (xh, xl, own), works = refs[38:41], refs[41 : 41 + len(CHUNKS)]
    high, low, dhv, dlv, panels, mine, raw, sems = refs[41 + len(CHUNKS) :]
    x, y, z, c = place()
    far = x >= 2
    copies = Copies(sems)
    for e in range(2):
        for h in range(2):
            copies.start(1, late[2 * e + h], raw.at[e, 512 * h : 512 * h + 512], far)
    fetch_sides(copies, 0, sides, panels)
    fetch_quarter(copies, 0, early, None, True, high, low)
    copies.start(2, dh, dhv)
    copies.start(2, dl, dlv)
    for k, ref in enumerate(second):
        copies.start(2, ref, mine, y == k)
    copies.wait(1)

    @pl.when(far)
    def _():
        for e in range(2):
            slot = 2 * lax.rem(x, 2) + (c if e == 0 else 1 - c)

            def step(i, _):
                rows = pl.ds(pl.multiple_of(i * 128, 128), 128)
                high[slot, rows, :], low[slot, rows, :] = split(raw[e, rows, :])
                return 0

            lax.fori_loop(0, 8, step, 0)

    copies.wait(0)

    def extra(j, lanes):
        copies.wait(2)
        d = slice(j * N, j * N + N)
        mine[:, lanes] -= mul3(dhv[:, d], dlv[:, d], xh[d, lanes], xl[d, lanes])

    solve_quarter(high, low, panels, xh, xl, WIDE, extra)
    own[...] = panels[z]
    for (o, n), work in zip(CHUNKS, works):
        work[...] = mine[:, o : o + n]


def partial_kernel(lh, ll, xh, xl, out, lhv, llv, xhv, xlv, sems):
    copies = Copies(sems)
    copies.start(0, xh, xhv)
    copies.start(0, xl, xlv)
    copies.start(0, lh.at[:, 0 : 4 * N], lhv)
    copies.start(0, ll.at[:, 0 : 4 * N], llv)
    copies.wait(0)

    def step(i, _):
        rows = pl.ds(pl.multiple_of(i * N, N), N)
        for o, n in TILES[WIDE]:
            lanes = slice(o, o + n)
            out[rows, lanes] = mul3(lhv[rows, :], llv[rows, :], xhv[:, lanes], xlv[:, lanes])
        return 0

    lax.fori_loop(0, 2, step, 0)


def second_kernel(start, wide):
    def kernel(*refs):
        early, late, (lh, ll), sides = refs[:24], refs[24:32], refs[32:34], refs[34:38]
        own_first, part = refs[38:40]
        outs = refs[40:44]
        high, low, lhv, llv, panels, result, xh, xl, sems = refs[44:]
        _, y, z, _ = place()
        copies = Copies(sems)
        fetch_sides(copies, 0, sides, panels)
        fetch_quarter(copies, 0, early, late, False, high, low)
        copies.start(2, own_first.at[:, start : start + wide], result.at[0])
        copies.start(2, lh.at[:, 4 * N : 8 * N], lhv)
        copies.start(2, ll.at[:, 4 * N : 8 * N], llv)
        for r in range(2):
            copies.start(2, part.at[r * N : r * N + N, start : start + wide], result.at[2 + r])
        copies.wait(0)

        def extra(j, lanes):
            copies.wait(2)
            d = slice(j * N, j * N + N)
            for r in range(2):
                rows = slice(r * N, r * N + N)
                result[2 + r, :, lanes] += mul3(lhv[rows, d], llv[rows, d], xh[d, lanes], xl[d, lanes])

        solve_quarter(high, low, panels, xh, xl, wide, extra)
        result[1] = panels[z]
        for k in range(4):
            outs[k][...] = result[lax.rem(y + k, 4)]

    return kernel


def last_kernel(start, wide):
    def kernel(mine, got0, got1, got2, got3, *refs):
        out, kept, sems = refs[-3:]
        _, y, _, _ = place()
        copies = Copies(sems)
        for chunk in range(4):
            lanes = slice(chunk * WIDE + start, chunk * WIDE + start + wide)
            copies.start(0, mine.at[:, lanes], kept.at[chunk], y >= 2)
        copies.wait(0)
        for k, got in enumerate((got0, got1, got2, got3)):
            chunk = lax.rem(y - k + 4, 4)

            @pl.when(y < 2)
            def _():
                kept[chunk] = got[...]

            @pl.when(y >= 2)
            def _():
                kept[chunk] = kept[chunk] - got[...]

        for chunk in range(4):
            lanes = slice(chunk * WIDE + start, chunk * WIDE + start + wide)
            copies.start(1, kept.at[chunk], out.at[:, lanes])
        copies.wait(1)

    return kernel


def send(value, axis, pairs):
    return lax.ppermute(value, axis, pairs)


def gather_x(a, b):
    back = [send(v, "col", along_x(1)) for v in (a, b)]
    front = [send(v, "col", along_x(3)) for v in (a, b)]
    far = [send(back[0], "col", along_x(1)), send(front[1], "col", along_x(3))]
    pieces = [a, b, *back, *front, *far]
    return pieces + [send(p, "col", CORES) for p in pieces]


def gather_x_whole(value):
    half = value.shape[0] // 2
    back = send(value, "col", along_x(1))
    front = send(value, "col", along_x(3))
    far = [send(back[:half], "col", along_x(1)), send(front[half:], "col", along_x(3))]
    pieces = [value, back, front, *far]
    return pieces + [send(p, "col", CORES) for p in pieces]


def gather_z(value):
    return [value] + [send(value, "row", along_z(k)) for k in (1, 2, 3)]


def work_on(integrals, factor):
    _, y, _, _ = place()
    bf = lambda *shape: sds(*shape, dtype=BF16)
    vf = lambda *shape: pltpu.VMEM(shape, F32)
    vb = lambda *shape: pltpu.VMEM(shape, BF16)
    sems = pltpu.SemaphoreType.DMA((64,))
    got = [send(factor, "row", along_y(k)) for k in (1, 2, 3)]
    chunks = [integrals[:, q * WIDE : (q + 1) * WIDE] for q in range(4)]
    mine = (chunks[0], chunks[1], *(jnp.where(y == 0, chunks[k], chunks[(k + 1) % 4]) for k in (1, 2, 3)))
    mine = lax.optimization_barrier(mine)
    came = [send(mine[k + 1], "row", along_y(k, (0, 1))) for k in (1, 2, 3)]
    shared, rest = call(sort_kernel, (sds(N, N), sds(3 * N, N)))(factor, *got)
    rest = gather_x_whole(rest)
    shared = call(invert_kernel, sds(N, N), [vf(2, 128, 128)])(shared)
    tri = gather_x(*call(stack_kernel, (sds(2 * N, N), sds(2 * N, N)))(*gather_z(shared)))
    side1 = jnp.where(y == 0, mine[0], jnp.where(y == 1, came[0], jnp.where(y == 2, came[1], came[2])))
    sides = gather_z(side1)
    side2 = (came[2], mine[1], came[0], came[1])
    dh, dl, lh, ll = call(
        prepare_rows_kernel,
        (bf(N, 4 * N), bf(N, 4 * N), bf(2 * N, 8 * N), bf(2 * N, 8 * N)),
        [vf(4, N, N), vf(4, 2 * N, N), vf(4, 2 * N, N), sems],
        ANYWHERE,
    )(*rest)
    early = call(split_kernel, (bf(2 * N, N),) * 24)(*tri[0:6], *tri[8:14])
    quarter = [vb(4, 4 * N, N), vb(4, 4 * N, N)]
    xh, xl, own, *works = call(
        first_kernel,
        (bf(4 * N, WIDE), bf(4 * N, WIDE), sds(N, WIDE)) + tuple(sds(N, n) for _, n in CHUNKS),
        quarter + [vb(N, 4 * N), vb(N, 4 * N), vf(4, N, WIDE), vf(N, WIDE), vf(2, 4 * N, N), sems],
        ANYWHERE,
    )(*early, *tri[6:8], *tri[14:16], dh, dl, *sides, *side2)
    late = call(split_kernel, (bf(2 * N, N),) * 8)(*tri[6:8], *tri[14:16])
    works = [gather_z(work) for work in works]
    part = call(
        partial_kernel,
        sds(2 * N, WIDE),
        [vb(2 * N, 4 * N), vb(2 * N, 4 * N), vb(4 * N, WIDE), vb(4 * N, WIDE), sems],
        ANYWHERE,
    )(lh, ll, xh, xl)
    out = ()
    for q, (o, n) in enumerate(CHUNKS):
        outs = call(
            second_kernel(o, n),
            (sds(N, n),) * 4,
            quarter
            + [vb(2 * N, 4 * N), vb(2 * N, 4 * N), vf(4, N, n), vf(4, N, n), vb(4 * N, n), vb(4 * N, n), sems],
            ANYWHERE,
        )(*early, *late, lh, ll, *works[q], own, part)
        got = [outs[0]] + [send(outs[k], "row", along_y(k)) for k in (1, 2, 3)]
        out = (finish(o, n, integrals, got, out),)
    return out[0]


def finish(start, wide, integrals, got, out):
    anywhere, inside = pl.BlockSpec(memory_space=ANYWHERE), pl.BlockSpec(memory_space=pltpu.VMEM)
    return pl.pallas_call(
        last_kernel(start, wide),
        out_shape=sds(*integrals.shape),
        in_specs=[anywhere] + [inside] * 4 + [anywhere] * len(out),
        out_specs=anywhere,
        scratch_shapes=[pltpu.VMEM((4, N, wide), F32), pltpu.SemaphoreType.DMA((8,))],
        input_output_aliases={5: 0} if out else {},
    )(integrals, *got, *out)


def solution(mesh):
    placed = (P("row", "col"), P("row", "col"))
    return jax.shard_map(work_on, mesh=mesh, in_specs=placed, out_specs=P("row", "col"), check_vma=False)
```

```python
import jax
import jax.numpy as jnp
from jax import lax
from jax.experimental import pallas as pl
from jax.experimental.pallas import tpu as pltpu
from jax.sharding import PartitionSpec as P


F32 = jnp.float32
BF16 = jnp.bfloat16
N = 256
WIDE = 640
ANYWHERE = pltpu.HBM
CHUNKS = ((0, 256), (256, 384))
TILES = {640: ((0, 256), (256, 256), (512, 128)), 384: ((0, 256), (256, 128)), 256: ((0, 256),)}


def along_y(k, sources=(0, 1, 2, 3)):
    return [(4 * y + z, 4 * ((y + k) % 4) + z) for y in sources for z in range(4)]


def along_z(k):
    return [(4 * y + z, 4 * y + (z + k) % 4) for y in range(4) for z in range(4)]


def along_x(k):
    return [(2 * x + c, 2 * ((x + k) % 4) + c) for x in range(4) for c in range(2)]


CORES = [(c, c ^ 1) for c in range(8)]


def place():
    row, col = lax.axis_index("row"), lax.axis_index("col")
    return col // 2, row // 4, row % 4, col % 2


def split(value):
    high = value.astype(BF16)
    return high, (value - high.astype(F32)).astype(BF16)


def mul(a, b):
    return lax.dot_general(a, b, (((1,), (0,)), ((), ())), preferred_element_type=F32)


def mul3(ah, al, bh, bl):
    both = mul(jnp.concatenate([ah, al], axis=0), bh)
    return both[: ah.shape[0]] + (mul(ah, bl) + both[ah.shape[0] :])


def call(kernel, outs, scratch=(), space=pltpu.VMEM, **kw):
    spec = pl.BlockSpec(memory_space=pltpu.VMEM)

    def run(*args):
        return pl.pallas_call(
            kernel,
            out_shape=outs,
            in_specs=[pl.BlockSpec(memory_space=space)] * len(args),
            out_specs=jax.tree.map(lambda _: spec, outs),
            scratch_shapes=scratch,
            **kw,
        )(*args)

    return run


class Copies:
    def __init__(self, sems):
        self.sems, self.used, self.by_key = sems, 0, {}

    def start(self, key, source, target, when=None):
        copy = pltpu.make_async_copy(source, target, self.sems.at[self.used])
        self.used += 1
        self.by_key.setdefault(key, []).append((copy, when))
        if when is None:
            copy.start()
        else:
            pl.when(when)(copy.start)

    def wait(self, key):
        for copy, when in self.by_key.pop(key, ()):
            if when is None:
                copy.wait()
            else:
                pl.when(when)(copy.wait)


def sds(*shape, dtype=F32):
    return jax.ShapeDtypeStruct(shape, dtype)


def sort_kernel(own, y1, y2, y3, shared, rest):
    x, y, _, _ = place()
    got = (own, y1, y2, y3)
    for row in range(4):
        for k in range(4):
            @pl.when(lax.rem(y - row + 4, 4) == k)
            def _():
                if row:
                    rest[(row - 1) * N : row * N, :] = got[k][...]
                if row < 2:
                    @pl.when((x < 2) if row == 0 else (x >= 2))
                    def _():
                        shared[...] = got[k][...]


def invert_kernel(block, out, strict):
    x, _, z, c = place()
    out[...] = block[...]

    @pl.when(z == 2 * lax.rem(x, 2) + c)
    def _():
        rows = lax.broadcasted_iota(jnp.int32, (128, 128), 0)
        cols = lax.broadcasted_iota(jnp.int32, (128, 128), 1)
        eye = rows == cols
        one = jnp.where(eye, 1.0, 0.0).astype(F32)
        scale_row, done = [], []
        for b in range(2):
            value = block[128 * b : 128 * b + 128, 128 * b : 128 * b + 128]
            scale = 1.0 / jnp.sum(jnp.where(eye, value, 0.0), axis=1, keepdims=True)
            strict[b] = jnp.where(rows > cols, value * scale, 0.0)
            scale_row.append(jnp.sum(jnp.where(eye, jnp.broadcast_to(scale, (128, 128)), 0.0), axis=0, keepdims=True))
            done.append([one[8 * t : 8 * t + 8, :] for t in range(16)])
        for k in range(127):
            first = (k + 1) // 8
            for b in range(2):
                line = jnp.broadcast_to(done[b][k // 8][k % 8 : k % 8 + 1, :], (8, 128))
                for t in range(first, 16):
                    left = strict[b, 8 * t : 8 * t + 8, :]
                    done[b][t] = done[b][t] - jnp.broadcast_to(left[:, k : k + 1], (8, 128)) * line
        for b in range(2):
            for t in range(16):
                at = 128 * b + 8 * t
                out[at : at + 8, 128 * b : 128 * b + 128] = done[b][t] * scale_row[b]


def stack_kernel(own, z1, z2, z3, a, b):
    a[0:256, :] = own[...]
    a[256:512, :] = z1[...]
    b[0:256, :] = z2[...]
    b[256:512, :] = z3[...]


def fetch_rows(copies, key, near, far, first_half, at, count, high, low):
    x, _, _, c = place()
    for e in range(2):
        for q, d in enumerate((0, 1, 3, 2)):
            there = lax.rem(x - d + 4, 4)
            slot = 2 * lax.rem(there, 2) + (c if e == 0 else 1 - c)
            when = (there < 2) if first_half else (there >= 2)
            for i, target in enumerate((high, low)):
                ref = far[2 * e + i] if d == 2 else near[6 * e + 2 * q + i].at[at : at + count]
                copies.start(key, ref, target.at[slot], when)


def fetch_sides(copies, key, sides, panels):
    _, _, z, _ = place()
    for k, ref in enumerate(sides):
        copies.start(key, ref, panels.at[lax.rem(z - k + 4, 4)])


def split_kernel(*refs):
    count = len(refs) // 3
    for k in range(count):
        def step(i, _):
            rows = pl.ds(pl.multiple_of(i * 128, 128), 128)
            refs[count + 2 * k][rows, :], refs[count + 2 * k + 1][rows, :] = split(refs[k][rows, :])
            return 0

        lax.fori_loop(0, refs[k].shape[0] // 128, step, 0)


def fetch_quarter(copies, key, early, late, first_half, high, low):
    x, _, _, c = place()
    for e in range(2):
        for q, d in enumerate((0, 1, 3, 2)):
            if d == 2 and late is None:
                continue
            there = lax.rem(x - d + 4, 4)
            slot = 2 * lax.rem(there, 2) + (c if e == 0 else 1 - c)
            when = (there < 2) if first_half else (there >= 2)
            pieces = late[4 * e :] if d == 2 else early[12 * e + 4 * q :]
            for h in range(2):
                for ref, target in zip(pieces[2 * h : 2 * h + 2], (high, low)):
                    copies.start(key, ref, target.at[slot, 512 * h : 512 * h + 512], when)


def solve_quarter(high, low, panels, xh, xl, wide, extra):
    _, _, z, _ = place()

    def block(i, j, r=0, q=0, rows=N, cols=N):
        at = pl.multiple_of(lax.rem(z - i + 4, 4) * N + r, 128)
        return high[j, pl.ds(at, rows), q : q + cols], low[j, pl.ds(at, rows), q : q + cols]

    def update(i, j, lanes):
        d = slice(j * N, j * N + N)
        panels[i, :, lanes] -= mul3(*block(i, j), xh[d, lanes], xl[d, lanes])

    def top(i, lanes):
        d = i * N
        value = mul3(*block(i, i, 0, 0, 128, 128), *split(panels[i, 0:128, lanes]))
        panels[i, 0:128, lanes] = value
        xh[d : d + 128, lanes], xl[d : d + 128, lanes] = split(value)

    def middle(i, lanes):
        d = slice(i * N, i * N + 128)
        panels[i, 128:256, lanes] -= mul3(*block(i, i, 128, 0, 128, 128), xh[d, lanes], xl[d, lanes])

    def bottom(i, lanes):
        d = i * N + 128
        value = mul3(*block(i, i, 128, 128, 128, 128), *split(panels[i, 128:256, lanes]))
        panels[i, 128:256, lanes] = value
        xh[d : d + 128, lanes], xl[d : d + 128, lanes] = split(value)

    tiles = [slice(o, o + n) for o, n in TILES[wide]]
    for i in range(4):
        spare = [lambda t, k=k: update(k, i - 1, t) for k in range(i + 1, 4) if i]
        if i:
            spare.append(lambda t: extra(i - 1, t))
        for k, step in enumerate((top, middle, bottom)):
            for lanes in tiles:
                if k == 0 and i:
                    update(i, i - 1, lanes)
                step(i, lanes)
            for work in spare[k : None if k == 2 else k + 1]:
                for lanes in tiles:
                    work(lanes)
    for lanes in tiles:
        extra(3, lanes)


def first_kernel(*refs):
    early, late, near, far_d = refs[:24], refs[24:28], refs[28:40], refs[40:44]
    sides, second, (xh, xl, own), works = refs[44:48], refs[48:52], refs[52:55], refs[55 : 55 + len(CHUNKS)]
    high, low, dhv, dlv, panels, mine, raw, sems = refs[55 + len(CHUNKS) :]
    x, y, z, c = place()
    far = x >= 2
    copies = Copies(sems)
    for e in range(2):
        for h in range(2):
            copies.start(1, late[2 * e + h], raw.at[e, 512 * h : 512 * h + 512], far)
    fetch_sides(copies, 0, sides, panels)
    fetch_quarter(copies, 0, early, None, True, high, low)
    fetch_rows(copies, 2, near, far_d, True, 0, N, dhv, dlv)
    for k, ref in enumerate(second):
        copies.start(2, ref, mine, y == k)
    copies.wait(1)

    @pl.when(far)
    def _():
        for e in range(2):
            slot = 2 * lax.rem(x, 2) + (c if e == 0 else 1 - c)

            def step(i, _):
                rows = pl.ds(pl.multiple_of(i * 128, 128), 128)
                high[slot, rows, :], low[slot, rows, :] = split(raw[e, rows, :])
                return 0

            lax.fori_loop(0, 8, step, 0)

    copies.wait(0)

    def extra(j, lanes):
        copies.wait(2)
        d = slice(j * N, j * N + N)
        mine[:, lanes] -= mul3(dhv[j], dlv[j], xh[d, lanes], xl[d, lanes])

    solve_quarter(high, low, panels, xh, xl, WIDE, extra)
    own[...] = panels[z]
    for (o, n), work in zip(CHUNKS, works):
        work[...] = mine[:, o : o + n]


def partial_kernel(*refs):
    near, far, (xh, xl), out = refs[:12], refs[12:16], refs[16:18], refs[18]
    lhv, llv, xhv, xlv, sems = refs[19:]
    copies = Copies(sems)
    copies.start(0, xh, xhv)
    copies.start(0, xl, xlv)
    fetch_rows(copies, 0, near, far, True, N, 2 * N, lhv, llv)
    copies.wait(0)

    def step(i, _):
        rows = pl.ds(pl.multiple_of(i * N, N), N)
        for o, n in TILES[WIDE]:
            lanes = slice(o, o + n)
            value = None
            for j in range(4):
                d = slice(j * N, j * N + N)
                part = mul3(lhv[j, rows, :], llv[j, rows, :], xhv[d, lanes], xlv[d, lanes])
                value = part if value is None else value + part
            out[rows, lanes] = value
        return 0

    lax.fori_loop(0, 2, step, 0)


def second_kernel(start, wide):
    def kernel(*refs):
        early, late, near, far_l = refs[:24], refs[24:32], refs[32:44], refs[44:48]
        sides, (own_first, part), outs = refs[48:52], refs[52:54], refs[54:58]
        high, low, lhv, llv, panels, result, xh, xl, sems = refs[58:]
        _, y, z, _ = place()
        copies = Copies(sems)
        fetch_sides(copies, 0, sides, panels)
        fetch_quarter(copies, 0, early, late, False, high, low)
        copies.start(2, own_first.at[:, start : start + wide], result.at[0])
        fetch_rows(copies, 2, near, far_l, False, N, 2 * N, lhv, llv)
        for r in range(2):
            copies.start(2, part.at[r * N : r * N + N, start : start + wide], result.at[2 + r])
        copies.wait(0)

        def extra(j, lanes):
            copies.wait(2)
            d = slice(j * N, j * N + N)
            for r in range(2):
                rows = slice(r * N, r * N + N)
                result[2 + r, :, lanes] += mul3(lhv[j, rows, :], llv[j, rows, :], xh[d, lanes], xl[d, lanes])

        solve_quarter(high, low, panels, xh, xl, wide, extra)
        result[1] = panels[z]
        for k in range(4):
            outs[k][...] = result[lax.rem(y + k, 4)]

    return kernel


def last_kernel(start, wide):
    def kernel(mine, got0, got1, got2, got3, *refs):
        out, kept, sems = refs[-3:]
        _, y, _, _ = place()
        copies = Copies(sems)
        for chunk in range(4):
            lanes = slice(chunk * WIDE + start, chunk * WIDE + start + wide)
            copies.start(0, mine.at[:, lanes], kept.at[chunk], y >= 2)
        copies.wait(0)
        for k, got in enumerate((got0, got1, got2, got3)):
            chunk = lax.rem(y - k + 4, 4)

            @pl.when(y < 2)
            def _():
                kept[chunk] = got[...]

            @pl.when(y >= 2)
            def _():
                kept[chunk] = kept[chunk] - got[...]

        for chunk in range(4):
            lanes = slice(chunk * WIDE + start, chunk * WIDE + start + wide)
            copies.start(1, kept.at[chunk], out.at[:, lanes])
        copies.wait(1)

    return kernel


def gather_x(a, b):
    back = [lax.ppermute(v, "col", along_x(1)) for v in (a, b)]
    front = [lax.ppermute(v, "col", along_x(3)) for v in (a, b)]
    far = [lax.ppermute(back[0], "col", along_x(1)), lax.ppermute(front[1], "col", along_x(3))]
    pieces = [a, b, *back, *front, *far]
    return pieces + [lax.ppermute(p, "col", CORES) for p in pieces]


def gather_rest(value):
    near = [value] + [lax.ppermute(value, "col", along_x(k)) for k in (1, 3)]
    far_d = lax.ppermute(value[:N], "col", along_x(2))
    far_l = lax.ppermute(value[N:], "col", along_x(2))
    other = [lax.ppermute(p, "col", CORES) for p in near]
    other_d, other_l = lax.ppermute(far_d, "col", CORES), lax.ppermute(far_l, "col", CORES)
    return [*near, *other], [far_d, other_d], [far_l, other_l]


def gather_z(value):
    return [value] + [lax.ppermute(value, "row", along_z(k)) for k in (1, 2, 3)]


def work_on(integrals, factor):
    _, y, _, _ = place()
    bf = lambda *shape: sds(*shape, dtype=BF16)
    vf = lambda *shape: pltpu.VMEM(shape, F32)
    vb = lambda *shape: pltpu.VMEM(shape, BF16)
    sems = pltpu.SemaphoreType.DMA((64,))
    got = [lax.ppermute(factor, "row", along_y(k)) for k in (1, 2, 3)]
    chunks = [integrals[:, q * WIDE : (q + 1) * WIDE] for q in range(4)]
    mine = (chunks[0], chunks[1], *(jnp.where(y == 0, chunks[k], chunks[(k + 1) % 4]) for k in (1, 2, 3)))
    mine = lax.optimization_barrier(mine)
    came = [lax.ppermute(mine[k + 1], "row", along_y(k, (0, 1))) for k in (1, 2, 3)]
    shared, rest = call(sort_kernel, (sds(N, N), sds(3 * N, N)))(factor, *got)
    near, far_d, far_l = gather_rest(rest)
    shared = call(invert_kernel, sds(N, N), [vf(2, 128, 128)])(shared)
    tri = gather_x(*call(stack_kernel, (sds(2 * N, N), sds(2 * N, N)))(*gather_z(shared)))
    side1 = jnp.where(y == 0, mine[0], jnp.where(y == 1, came[0], jnp.where(y == 2, came[1], came[2])))
    sides = gather_z(side1)
    side2 = (came[2], mine[1], came[0], came[1])
    rows = call(split_kernel, (bf(3 * N, N),) * 12 + (bf(N, N),) * 4)(*near, *far_d)
    near, far_d = rows[:12], rows[12:]
    early = call(split_kernel, (bf(2 * N, N),) * 24)(*tri[0:6], *tri[8:14])
    quarter = [vb(4, 4 * N, N), vb(4, 4 * N, N)]
    xh, xl, own, *works = call(
        first_kernel,
        (bf(4 * N, WIDE), bf(4 * N, WIDE), sds(N, WIDE)) + tuple(sds(N, n) for _, n in CHUNKS),
        quarter + [vb(4, N, N), vb(4, N, N), vf(4, N, WIDE), vf(N, WIDE), vf(2, 4 * N, N), sems],
        ANYWHERE,
    )(*early, *tri[6:8], *tri[14:16], *near, *far_d, *sides, *side2)
    late = call(split_kernel, (bf(2 * N, N),) * 12)(*tri[6:8], *tri[14:16], *far_l)
    late, far_l = late[:8], late[8:]
    works = [gather_z(work) for work in works]
    part = call(
        partial_kernel,
        sds(2 * N, WIDE),
        [vb(4, 2 * N, N), vb(4, 2 * N, N), vb(4 * N, WIDE), vb(4 * N, WIDE), sems],
        ANYWHERE,
    )(*near, *far_l, xh, xl)
    out = ()
    for q, (o, n) in enumerate(CHUNKS):
        outs = call(
            second_kernel(o, n),
            (sds(N, n),) * 4,
            quarter
            + [vb(4, 2 * N, N), vb(4, 2 * N, N), vf(4, N, n), vf(4, N, n), vb(4 * N, n), vb(4 * N, n), sems],
            ANYWHERE,
        )(*early, *late, *near, *far_l, *works[q], own, part)
        got = [outs[0]] + [lax.ppermute(outs[k], "row", along_y(k)) for k in (1, 2, 3)]
        out = (finish(o, n, integrals, got, out),)
    return out[0]


def finish(start, wide, integrals, got, out):
    anywhere, inside = pl.BlockSpec(memory_space=ANYWHERE), pl.BlockSpec(memory_space=pltpu.VMEM)
    return pl.pallas_call(
        last_kernel(start, wide),
        out_shape=sds(*integrals.shape),
        in_specs=[anywhere] + [inside] * 4 + [anywhere] * len(out),
        out_specs=anywhere,
        scratch_shapes=[pltpu.VMEM((4, N, wide), F32), pltpu.SemaphoreType.DMA((8,))],
        input_output_aliases={5: 0} if out else {},
    )(integrals, *got, *out)


def solution(mesh):
    placed = (P("row", "col"), P("row", "col"))
    return jax.shard_map(work_on, mesh=mesh, in_specs=placed, out_specs=P("row", "col"), check_vma=False)
```
